32 devices in a mesh: groups: 2 (over y), shard: 2 (over x), expert: 4 (over z), section: 2 (over core).
Axes of the slice: x: 2, y: 2, z: 4, core: 2. Of those that a mesh axis runs over, the one named last changes fastest.
Arguments:
- tokens: bfloat16 [2, 512, 6144], P(None, ('groups', 'shard', 'expert')), parts along dimension 1, may hold values from -6 to 6
- norm_gain: float32 [2, 6144], P('section'), may hold values from 0.5 to 2
- route_ids: int32 [2, 2, 512, 2], P('section', None, ('groups', 'shard', 'expert')), parts along dimension 2, may hold values from 0 to 3, all different within a row; in each aligned block of 32 rows (0 to 31, 32 to 63, ..., all dimensions but the last counted through in order) at most 18 rows name the same one
- route_weights: float32 [2, 2, 512, 2], P('section', None, ('groups', 'shard', 'expert')), parts along dimension 2, may hold values from 0.25 to 1
- gate_blocks: bfloat16 [2, 4, 64, 1, 128, 128], P('section', 'expert', 'shard'), may hold values from -0.5 to 0.5
- up_blocks: bfloat16 [2, 4, 64, 1, 128, 128], P('section', 'expert', 'shard'), may hold values from -0.5 to 0.5
- down_blocks: bfloat16 [2, 4, 64, 1, 128, 128], P('section', 'expert', 'shard'), may hold values from -0.4375 to 0.4375
- gate_rows: int32 [2, 4, 64, 1], P('section', 'expert', 'shard'), may hold values from 0 to 47
- down_cols: int32 [2, 4, 64, 1], P('section', 'expert', 'shard'), may hold values from 0 to 47
Outputs:
- hidden_states: bfloat16 [2, 2, 512, 6144], P('section', None, ('groups', 'shard', 'expert')), parts along dimension 2
The draws below stay inside these ranges and needn't reach their ends.
There are 2 independent parts, one for each index of `groups`. The reference program is written for one: setup_inputs(seed, part) draws one part's arguments, and reference() takes and returns one part's arrays. A program takes and returns all parts, laid end to end along the dimension named above; an argument that names none is the same for every part. Nothing has to cross between parts.
Inputs may be any that keep to these rules, and one draw needn't show every extreme that they name: `route_ids`: the 2 experts of a token differ; among the 32 tokens of one device, one micro-batch and one layer, no expert is named by more than 18 tokens, a bound that some block reaches of them.
All inputs are finite; a program needn't handle non-finite values.
Results may differ from the reference program's by a relative error of at most 0.0064.
Values may be sent and summed in bfloat16 or wider, within the bound.
A program may use at most 64 MiB of HBM per device.

```python
import math
import jax
import jax.numpy as jnp
import numpy as np
from jax import lax

D = 6144
FF = 8192
BLK = 128
KEEP = 1
TOP = 2
LAYERS = 2
MICRO = 2
TOK_MB = 32
EXPERTS = 4
CAP = 18
TOKENS = 256


def pick_blocks(key):
    block_rows = D // BLK
    scores = jax.random.randint(key, (LAYERS, EXPERTS, FF // BLK, block_rows), 0, 1 << 20, dtype=jnp.int32)
    scores = scores * block_rows + jnp.arange(block_rows, dtype=jnp.int32)
    return lax.top_k(scores, KEEP)[1].astype(jnp.int32)


def draw_gate_rows(key, part):
    return pick_blocks(jax.random.fold_in(key, 11))


def draw_down_cols(key, part):
    return pick_blocks(jax.random.fold_in(key, 23))


def block_scale(key, extent, pieces, smallest, high):
    factor_of, own = 1.0, jax.random.fold_in(key, 6)
    for position, shards_of in pieces:
        draws = jnp.exp(jax.random.uniform(jax.random.fold_in(own, position), (shards_of,), jnp.float32, smallest / len(pieces), high / len(pieces)))
        factor_of = factor_of * jnp.repeat(draws, extent[position] // shards_of).reshape([-1 if axis == position else 1 for axis in range(len(extent))])
    return factor_of


def assign_block(rng, own, number, rows, number_of, top, most, slope):
    order = jax.random.permutation(rng, number_of)
    packed, ordinary = load_shares(number_of, rows * top, most, slope, True), load_shares(number_of, rows * top, most, slope, False)
    places = jnp.arange(number_of)

    def named(lengths, offset_by):
        used = int((lengths > 0).sum())
        fixed = max(1, used // 4)
        shifted = fixed + (places - fixed + offset_by * (used - fixed)) % max(1, number_of - fixed)
        return jnp.zeros((number_of,), jnp.int32).at[order[jnp.where(places < fixed, places, shifted)]].set(jnp.asarray(lengths, jnp.int32))

    lengths = jnp.where(number % 4 == 0, named(packed, number // 4), named(ordinary, number - number // 4 - 1))
    mixed = jax.random.permutation(jax.random.fold_in(own, 3), number_of)
    donor, sink = mixed[0:number_of // 2 * 2:2], mixed[1:number_of // 2 * 2:2]
    room = jnp.minimum(lengths[donor] - 1, most - lengths[sink]) // 2
    room = jnp.where((donor == order[0]) | (sink == order[0]) | (lengths[sink] == 0), 0, jnp.maximum(room, 0))
    shifted = jax.random.randint(jax.random.fold_in(own, 4), (number_of // 2,), 0, 1 << 20) % (room + 1)
    lengths = lengths.at[donor].add(-shifted).at[sink].add(shifted)
    labels = jnp.searchsorted(jnp.cumsum(lengths), jnp.arange(rows * top), side="right").astype(jnp.int32)
    listing = labels.reshape(top, rows).T
    listing = listing[jax.random.permutation(jax.random.fold_in(own, 1), rows)]
    offset_by = jax.random.randint(jax.random.fold_in(own, 2), (rows, 1), 0, top)
    return jnp.take_along_axis(listing, (jnp.arange(top)[None, :] + offset_by) % top, axis=1)


def load_shares(count, total, reach, lean, full):
    weights = [(1 << 20) // math.isqrt(standing ** lean) + 1 for standing in range(1, count + 1)]
    largest = reach if full else min(reach, max(-(-total // count), total * weights[0] // sum(weights)))
    least = 1 if total - largest >= count - 1 else 0
    holding, rest = [largest] + [least] * (count - 1), total - largest - least * (count - 1)
    while rest > 0:
        free = [i for i in range(1, count) if holding[i] < largest] or [i for i in range(1, count) if holding[i] < reach]
        whole, remaining = sum([weights[i] for i in free]), rest
        for i in free:
            addition = min(reach - holding[i], max(1, remaining * weights[i] // whole), rest)
            holding[i] = holding[i] + addition
            rest = rest - addition
    return np.array(holding)


def gaussian(rng, shape, scale, most, pieces=(), held_as=jnp.bfloat16):
    array = jax.random.normal(rng, shape, jnp.float32) * scale
    if len(pieces) > 0:
        array = block_scale(rng, shape, pieces, -0.22, 0.18) * array
    return jnp.clip(array, min=-most, max=most).astype(held_as)


def setup_inputs(seed: int = 0, part: int = 0) -> dict:
    arg_keys = jax.random.split(jax.random.key(seed), 10)
    own_keys = jax.random.split(jax.random.fold_in(arg_keys[9], part), 10)
    tokens = gaussian(own_keys[0], (MICRO, TOKENS, D), 1.0, 6.0, ((1, 8),))
    norm_gain = jnp.clip(jnp.exp(math.log(2.0) - 1.3862944 * jax.random.uniform(arg_keys[1], (LAYERS, D), jnp.float32) ** block_scale(arg_keys[1], (LAYERS, D), ((0, 2),), -0.2, 0.2)), 0.5, 2.0)
    route_ids_keys = jax.random.split(jax.random.fold_in(own_keys[2], 1), LAYERS * MICRO * TOKENS // TOK_MB)
    route_ids_turns = jax.random.permutation(jax.random.fold_in(own_keys[2], 3), LAYERS * MICRO * TOKENS // TOK_MB)
    route_ids = jax.vmap(lambda own, number: assign_block(jax.random.fold_in(own_keys[2], 2), own, number, TOK_MB, EXPERTS, TOP, CAP, 2))(route_ids_keys, route_ids_turns).reshape((LAYERS, MICRO, TOKENS, TOP))
    route_weights = jnp.clip(0.25 + 0.75 * jax.random.uniform(own_keys[3], (LAYERS, MICRO, TOKENS, TOP), jnp.float32) ** block_scale(own_keys[3], (LAYERS, MICRO, TOKENS, TOP), ((0, 2), (2, 8)), -0.2, 0.2), 0.25, 1.0)
    gate_blocks = gaussian(arg_keys[4], (LAYERS, EXPERTS, FF // BLK, KEEP, BLK, BLK), (KEEP * BLK) ** -0.5, 0.5, ((0, 2), (1, 4), (2, 2)))
    up_blocks = gaussian(arg_keys[5], (LAYERS, EXPERTS, FF // BLK, KEEP, BLK, BLK), (KEEP * BLK) ** -0.5, 0.5, ((0, 2), (1, 4), (2, 2)))
    down_blocks = gaussian(arg_keys[6], (LAYERS, EXPERTS, FF // BLK, KEEP, BLK, BLK), (FF * KEEP * BLK // D) ** -0.5, 0.4375, ((0, 2), (1, 4), (2, 2)))
    gate_rows = draw_gate_rows(jax.random.fold_in(arg_keys[9], 71), part)
    down_cols = draw_down_cols(jax.random.fold_in(arg_keys[9], 71), part)
    return dict(tokens=tokens, norm_gain=norm_gain, route_ids=route_ids, route_weights=route_weights, gate_blocks=gate_blocks, up_blocks=up_blocks, down_blocks=down_blocks, gate_rows=gate_rows, down_cols=down_cols)


def normalize(values, gain_row):
    wide = values.astype(jnp.float32)
    scale = lax.rsqrt(lax.optimization_barrier(jnp.mean(wide * wide, axis=-1, keepdims=True)) + 1e-05)
    return (wide * scale * gain_row).astype(jnp.bfloat16)

def expert_rows(inputs, gate_w, up_w, down_w, row_index, col_index):
    row_total = inputs.shape[0]
    block_size = gate_w.shape[-1]
    block_rows = inputs.shape[1] // block_size
    blocks = inputs.reshape(row_total, block_rows, block_size)
    picked = jnp.take(blocks, row_index.reshape(-1), axis=1)
    picked = picked.reshape(row_total, row_index.shape[0], row_index.shape[1], block_size).astype(jnp.float32)
    gate = jnp.einsum('rckd,ckdf->rcf', picked, gate_w.astype(jnp.float32), precision=lax.Precision.HIGHEST)
    up_val = jnp.einsum('rckd,ckdf->rcf', picked, up_w.astype(jnp.float32), precision=lax.Precision.HIGHEST)
    hidden = (jax.nn.silu(gate) * up_val).astype(jnp.bfloat16).astype(jnp.float32)
    result = jnp.zeros((row_total, block_rows, block_size), jnp.float32)
    for kept in range(row_index.shape[1]):
        part_out = jnp.einsum('rcf,cfo->rco', hidden, down_w[:, kept].astype(jnp.float32), precision=lax.Precision.HIGHEST)
        result = result.at[:, col_index[:, kept].astype(jnp.int32)].add(part_out)
    return result.reshape(row_total, block_rows * block_size).astype(jnp.bfloat16)

def reference(tokens, norm_gain, route_ids, route_weights, gate_blocks, up_blocks, down_blocks, gate_rows, down_cols):
    limit = min(TOKENS, TOKENS // TOK_MB * CAP)
    state = tokens
    layer_outputs = []
    for layer in range(LAYERS):
        results = []
        for micro_index in range(MICRO):
            current = state[micro_index]
            normed = normalize(current, norm_gain[layer])
            chosen_ids = route_ids[layer, micro_index]
            chosen_weights = route_weights[layer, micro_index]
            total = current.astype(jnp.float32)
            for expert_index in range(EXPERTS):
                hits = chosen_ids == expert_index
                chosen = jnp.any(hits, axis=1)
                positions = jnp.nonzero(chosen, size=limit, fill_value=0)[0].astype(jnp.int32)
                valid = jnp.arange(limit, dtype=jnp.int32) < jnp.sum(chosen.astype(jnp.int32))
                weight_all = lax.optimization_barrier(jnp.sum(jnp.where(hits, chosen_weights, jnp.zeros((), chosen_weights.dtype)), axis=1))
                weight_rows = jnp.where(valid, weight_all[positions], jnp.zeros((), chosen_weights.dtype))
                produced = expert_rows(normed[positions], gate_blocks[layer, expert_index], up_blocks[layer, expert_index], down_blocks[layer, expert_index], gate_rows[layer, expert_index], down_cols[layer, expert_index])
                total = total.at[positions].add(weight_rows[:, None] * produced.astype(jnp.float32))
            results.append(total.astype(jnp.bfloat16))
        state = jnp.stack(results)
        layer_outputs.append(state)
    return jnp.stack(layer_outputs)
```

```python
import functools

import jax
import jax.numpy as jnp
from jax import lax
from jax.experimental import pallas as pl
from jax.experimental.pallas import tpu as pltpu
from jax.sharding import PartitionSpec as P

TOP = 2
EPS = 1e-05
BF16 = jnp.bfloat16
F32 = jnp.float32


def layer_kernel(
    dims,
    tokens, gain, disp, comb, gate_hbm, up_hbm, down_hbm, meta_hbm,
    out,
    held, normed, wide, send, recv, parts, ret_send, ret_recv, weights, meta_v, meta_s,
    tok_sem, hand_sem, own_sem, meta_own_sem, meta_send_sem, meta_recv_sem, meta_copy_sem,
    wx_send, wx_recv, wy_send, wy_recv, disp_send, disp_recv, disp_self,
    back_send, back_recv, back_self, go_sem,
):
    micro, rows, blocks, blk, cap, experts, shards, groups, sections, n_blk = dims
    slots = experts * cap
    me_g, me_s = lax.axis_index("groups"), lax.axis_index("shard")
    me_e, me_l = lax.axis_index("expert"), lax.axis_index("section")
    sizes = {"groups": groups, "shard": shards, "expert": experts, "section": sections}
    place = {"groups": me_g, "shard": me_s, "expert": me_e, "section": me_l}
    half = n_blk // groups
    cuts = 2 if half % 2 == 0 else 1
    step = half // cuts
    sources = (gate_hbm, up_hbm, down_hbm)

    def remote(src, dst, ssem, rsem, axis, index):
        return pltpu.make_async_remote_copy(
            src_ref=src, dst_ref=dst, send_sem=ssem, recv_sem=rsem,
            device_id={axis: index}, device_id_type=pl.DeviceIdType.MESH,
        )

    def peer(axis, by):
        return lax.rem(place[axis] + by, sizes[axis])

    own = [
        pltpu.make_async_copy(sources[a], weights.at[a, me_s], own_sem.at[a]) for a in range(3)
    ]
    for copy in own:
        copy.start()
    meta_own = pltpu.make_async_copy(meta_hbm, meta_v.at[me_s], meta_own_sem)
    meta_own.start()

    barrier = pltpu.get_barrier_semaphore()
    for axis in ("groups", "shard", "expert", "section"):
        for by in range(1, sizes[axis]):
            pl.semaphore_signal(
                barrier, inc=1, device_id={axis: peer(axis, by)},
                device_id_type=pl.DeviceIdType.MESH,
            )
    pl.semaphore_wait(barrier, sum(n - 1 for n in sizes.values()))

    def token_copy(m):
        return pltpu.make_async_copy(tokens.at[m], held.at[m], tok_sem.at[m])

    def hand_copy(m):
        return remote(
            out.at[m], held.at[m], hand_sem.at[0, m], hand_sem.at[1, m], "section",
            peer("section", 1),
        )

    def part(group, a, k, shard):
        return weights.at[a, shard, pl.ds(group * half + k * step, step)]

    def over_shard(a, k, by):
        i = k * 3 + a
        src = sources[a].at[pl.ds(me_g * half + k * step, step)]
        return remote(
            src, part(me_g, a, k, me_s), wx_send.at[i, by], wx_recv.at[i, by], "shard",
            peer("shard", by),
        )

    def over_groups(a, k, by, hop):
        i = k * 3 + a
        spot = part(me_g, a, k, peer("shard", shards - by))
        return remote(
            spot, spot, wy_send.at[i, by, hop], wy_recv.at[i, by, hop], "groups",
            peer("groups", hop),
        )

    def meta_over_shard(by):
        return remote(
            meta_hbm, meta_v.at[me_s], meta_send_sem.at[by], meta_recv_sem.at[by], "shard",
            peer("shard", by),
        )

    order = [(a, k, by) for k in range(cuts) for a in range(3) for by in range(1, shards)]

    def start_weights():
        for by in range(1, shards):
            meta_over_shard(by).start()
        for a, k, by in order:
            over_shard(a, k, by).start()

    def relay_weights():
        for a, k, by in order:
            over_shard(a, k, by).wait_recv()
            for hop in range(1, groups):
                over_groups(a, k, by, hop).start()

    def finish_weights():
        for by in range(1, shards):
            meta_over_shard(by).wait()
        for a, k, by in order:
            over_shard(a, k, by).wait_send()
            for hop in range(1, groups):
                over_groups(a, k, by, hop).wait()

    def chunk_out(m, by):
        return remote(
            send.at[m, peer("expert", by)], recv.at[m, me_e], disp_send.at[m, by],
            disp_recv.at[m, by], "expert", peer("expert", by),
        )

    def chunk_self(m):
        return pltpu.make_async_copy(send.at[m, me_e], recv.at[m, me_e], disp_self.at[m])

    def chunk_back(m, by):
        return remote(
            ret_send.at[m, peer("expert", by)], ret_recv.at[m, me_e], back_send.at[m, by],
            back_recv.at[m, by], "expert", peer("expert", by),
        )

    def back_own(m):
        return pltpu.make_async_copy(ret_send.at[m, me_e], ret_recv.at[m, me_e], back_self.at[m])

    far_first = sorted(range(1, experts), key=lambda by: abs(by - experts // 2))

    def lanes(r):
        return pl.ds(pl.multiple_of(r * blk, blk), blk)

    def strided(r):
        return pl.ds(r, slots, stride=blocks)

    def dispatch(m):
        values = held[m].astype(F32)
        scale = lax.rsqrt(jnp.mean(values * values, axis=-1, keepdims=True) + EPS)
        normed[...] = (values * scale * gain[...]).astype(BF16)

        @pl.loop(0, blocks, unroll=8)
        def _(r):
            wide[strided(r), :] = jnp.dot(
                disp[m], normed[:, lanes(r)], preferred_element_type=F32
            )

        for e in range(experts):
            send[m, e] = wide[pl.ds(e * cap * blocks, cap * blocks), :].astype(BF16)
        for by in far_first:
            chunk_out(m, by).start()
        chunk_self(m).start()

    def shard_part(s):
        several = min(8, n_blk)

        @pl.loop(0, n_blk // several)
        def _(q):
            products = []
            for u in range(several):
                c = q * several + u
                x = wide[strided(meta_s[s, 0, c]), :].astype(BF16)
                gate = jnp.dot(x, weights[0, s, c], preferred_element_type=F32)
                up = jnp.dot(x, weights[1, s, c], preferred_element_type=F32)
                hidden = (gate / (1.0 + jnp.exp(-gate)) * up).astype(BF16)
                products.append(jnp.dot(hidden, weights[2, s, c], preferred_element_type=F32))
            for u in range(several):
                c = q * several + u
                parts[s, c] = products[u] + parts[s, meta_s[s, 0, n_blk + c]]

    def expert_part(m, first):
        for by in range(1, experts):
            chunk_out(m, by).wait()
        chunk_self(m).wait()
        for e in range(experts):
            wide[pl.ds(e * cap * blocks, cap * blocks), :] = recv[m, e].astype(F32)
        if first:
            for copy in own:
                copy.wait()
            finish_weights()
            meta_own.wait()
            load = pltpu.make_async_copy(meta_v, meta_s, meta_copy_sem)
            load.start()
            load.wait()

        @pl.loop(0, shards)
        def _(s):
            shard_part(s)

        @pl.loop(0, blocks, unroll=4)
        def _(j):
            total = parts[0, meta_s[0, 0, 2 * n_blk + j]]
            for s in range(1, shards):
                total = total + parts[s, meta_s[s, 0, 2 * n_blk + j]]
            wide[strided(j), :] = total

        for e in range(experts):
            ret_send[m, e] = wide[pl.ds(e * cap * blocks, cap * blocks), :].astype(BF16)
        for by in far_first:
            chunk_back(m, by).start()
        back_own(m).start()

    def combine(m):
        for by in range(1, experts):
            chunk_back(m, by).wait()
        back_own(m).wait()
        for e in range(experts):
            wide[pl.ds(e * cap * blocks, cap * blocks), :] = ret_recv[m, e].astype(F32)

        @pl.loop(0, blocks, unroll=8)
        def _(r):
            mixed = jnp.dot(
                comb[m], wide[strided(r), :], preferred_element_type=F32,
                precision=lax.Precision.HIGHEST,
            )
            out[m, :, lanes(r)] = (held[m, :, lanes(r)].astype(F32) + mixed).astype(BF16)

    for s in range(shards):
        parts[s, n_blk] = jnp.zeros_like(parts[s, n_blk])

    @pl.when(me_l == 0)
    def _():
        for m in range(micro):
            token_copy(m).start()
        start_weights()
        for m in range(micro):
            token_copy(m).wait()
            dispatch(m)
        relay_weights()

    @pl.when(me_l > 0)
    def _():
        pl.semaphore_wait(go_sem, 1)
        start_weights()
        relay_weights()

    @pl.when(me_l < sections - 1)
    def _():
        pl.semaphore_signal(
            go_sem, inc=1, device_id={"section": peer("section", 1)},
            device_id_type=pl.DeviceIdType.MESH,
        )

    @pl.when(me_l > 0)
    def _():
        for m in range(micro):
            hand_copy(m).wait_recv()
            dispatch(m)

    for m in range(micro):
        expert_part(m, m == 0)
    for m in range(micro):
        combine(m)

        @pl.when(me_l < sections - 1)
        def _():
            hand_copy(m).start()

    @pl.when(me_l < sections - 1)
    def _():
        for m in range(micro):
            hand_copy(m).wait_send()


def body(
    sizes,
    tokens,
    norm_gain,
    route_ids,
    route_weights,
    gate_blocks,
    up_blocks,
    down_blocks,
    gate_rows,
    down_cols,
):
    groups, shards, experts, sections = sizes
    micro, rows, width = tokens.shape
    n_blk, blk = gate_blocks.shape[2], gate_blocks.shape[-1]
    blocks = width // blk
    cap = min(rows, max(rows * 9 // 16, rows * TOP // experts + 2))
    slots = experts * cap

    ids, mix = route_ids[0], route_weights[0]
    named = ids[..., None] == jnp.arange(experts, dtype=jnp.int32)
    hit = jnp.any(named, axis=2)
    amount = jnp.sum(jnp.where(named, mix[..., None], 0.0), axis=2)
    earlier = jnp.arange(rows)[None, :] < jnp.arange(rows)[:, None]
    ahead = jnp.sum(
        jnp.where(earlier[None, :, :, None] & hit[:, None, :, :], 1, 0).astype(jnp.int32), axis=2
    )
    fits = hit[..., None] & (ahead[..., None] == jnp.arange(cap, dtype=jnp.int32))
    fits = fits.reshape(micro, rows, slots)
    comb = jnp.where(fits, jnp.repeat(amount, cap, axis=2), 0.0)
    disp = jnp.swapaxes(fits, 1, 2).astype(BF16)

    cols = down_cols[0, 0, :, 0]
    number = jnp.arange(n_blk, dtype=jnp.int32)
    same = (cols[:, None] == cols[None, :]) & (number[None, :] < number[:, None])
    before = jnp.max(jnp.where(same, number[None, :], -1), axis=1)
    before = jnp.where(before < 0, n_blk, before)
    here = cols[None, :] == jnp.arange(blocks, dtype=jnp.int32)[:, None]
    last = jnp.max(jnp.where(here, number[None, :], -1), axis=1)
    last = jnp.where(last < 0, n_blk, last)
    meta = jnp.concatenate([gate_rows[0, 0, :, 0], before, last])
    meta_width = -(-meta.shape[0] // 128) * 128
    meta = jnp.pad(meta, (0, meta_width - meta.shape[0]))[None]

    half = n_blk // groups
    pieces = 3 * (2 if half % 2 == 0 else 1)
    dims = (micro, rows, blocks, blk, cap, experts, shards, groups, sections, n_blk)
    dma = pltpu.SemaphoreType.DMA
    chunk = (micro, experts, cap * blocks, blk)
    vmem, anywhere = pl.BlockSpec(memory_space=pltpu.VMEM), pl.BlockSpec(memory_space=pl.ANY)
    out = pl.pallas_call(
        functools.partial(layer_kernel, dims),
        out_shape=jax.ShapeDtypeStruct((micro, rows, width), BF16),
        in_specs=[anywhere, vmem, vmem, vmem, anywhere, anywhere, anywhere, anywhere],
        out_specs=vmem,
        scratch_shapes=[
            pltpu.VMEM((micro, rows, width), BF16),
            pltpu.VMEM((rows, width), BF16),
            pltpu.VMEM((slots * blocks, blk), F32),
            pltpu.VMEM(chunk, BF16),
            pltpu.VMEM(chunk, BF16),
            pltpu.VMEM((shards, n_blk + 1, slots, blk), F32),
            pltpu.VMEM(chunk, BF16),
            pltpu.VMEM(chunk, BF16),
            pltpu.VMEM((3, shards, n_blk, blk, blk), BF16),
            pltpu.VMEM((shards, 1, meta_width), jnp.int32),
            pltpu.SMEM((shards, 1, meta_width), jnp.int32),
            dma((micro,)),
            dma((2, micro)),
            dma((3,)),
            dma,
            dma((shards,)),
            dma((shards,)),
            dma,
            dma((pieces, shards)),
            dma((pieces, shards)),
            dma((pieces, shards, groups)),
            dma((pieces, shards, groups)),
            dma((micro, experts)),
            dma((micro, experts)),
            dma((micro,)),
            dma((micro, experts)),
            dma((micro, experts)),
            dma((micro,)),
            pltpu.SemaphoreType.REGULAR,
        ],
        compiler_params=pltpu.CompilerParams(
            collective_id=0, has_side_effects=True, vmem_limit_bytes=56 * 1024 * 1024
        ),
    )(
        tokens, norm_gain, disp, comb,
        gate_blocks.reshape(n_blk, blk, blk), up_blocks.reshape(n_blk, blk, blk),
        down_blocks.reshape(n_blk, blk, blk), meta,
    )
    return out[None]


def solution(mesh):
    sizes = tuple(mesh.shape[name] for name in ("groups", "shard", "expert", "section"))
    in_specs = (
        P(None, ("groups", "shard", "expert"), None),
        P("section", None),
        P("section", None, ("groups", "shard", "expert"), None),
        P("section", None, ("groups", "shard", "expert"), None),
        P("section", "expert", "shard", None, None, None),
        P("section", "expert", "shard", None, None, None),
        P("section", "expert", "shard", None, None, None),
        P("section", "expert", "shard", None),
        P("section", "expert", "shard", None),
    )
    out_specs = P("section", None, ("groups", "shard", "expert"), None)
    return jax.shard_map(
        functools.partial(body, sizes), mesh=mesh, in_specs=in_specs, out_specs=out_specs,
        check_vma=False,
    )
```

```python
import functools
import math

import jax
import jax.numpy as jnp
from jax import lax
from jax.experimental import pallas as pl
from jax.experimental.pallas import tpu as pltpu
from jax.sharding import PartitionSpec as P

TOP = 2
EPS = 1e-05
BF16 = jnp.bfloat16
F32 = jnp.float32


def layer_kernel(
    dims,
    tokens, gain, ids, mix, gate_hbm, up_hbm, down_hbm, rows_in, cols_in,
    out,
    held, disp, comb, meta_here, normed, wide, send, recv, parts, ret_send, ret_recv, weights, meta_v, meta_s,
    tok_sem, hand_sem, own_sem, meta_own_sem, meta_send_sem, meta_recv_sem, meta_copy_sem,
    wx_send, wx_recv, wy_send, wy_recv, disp_send, disp_recv, disp_self,
    back_send, back_recv, back_self, go_sem,
):
    micro, rows, blocks, blk, cap, experts, shards, groups, sections, n_blk = dims
    slots = experts * cap
    me_g, me_s = lax.axis_index("groups"), lax.axis_index("shard")
    me_e, me_l = lax.axis_index("expert"), lax.axis_index("section")
    sizes = {"groups": groups, "shard": shards, "expert": experts, "section": sections}
    place = {"groups": me_g, "shard": me_s, "expert": me_e, "section": me_l}
    half = n_blk // groups
    cuts = math.gcd(half, 4)
    step = half // cuts
    sources = (gate_hbm, up_hbm, down_hbm)

    def remote(src, dst, ssem, rsem, axis, index):
        return pltpu.make_async_remote_copy(
            src_ref=src, dst_ref=dst, send_sem=ssem, recv_sem=rsem,
            device_id={axis: index}, device_id_type=pl.DeviceIdType.MESH,
        )

    def peer(axis, by):
        return lax.rem(place[axis] + by, sizes[axis])

    own = [
        pltpu.make_async_copy(sources[a], weights.at[a, me_s], own_sem.at[a]) for a in range(3)
    ]
    for copy in own:
        copy.start()
    meta_own = pltpu.make_async_copy(meta_here, meta_v.at[me_s], meta_own_sem)

    barrier = pltpu.get_barrier_semaphore()
    for axis in ("groups", "shard", "expert", "section"):
        for by in range(1, sizes[axis]):
            pl.semaphore_signal(
                barrier, inc=1, device_id={axis: peer(axis, by)},
                device_id_type=pl.DeviceIdType.MESH,
            )

    def arrival(c):
        group = sum((c >= g * half).astype(jnp.int32) for g in range(1, groups))
        within = c - group * half
        k = sum((within >= i * step).astype(jnp.int32) for i in range(1, cuts))
        return k * (groups - 1) * step + group * step + within

    def iota(shape, axis):
        return lax.broadcasted_iota(jnp.int32, shape, axis)

    cols = cols_in[...]
    cols_down = jnp.transpose(jnp.broadcast_to(cols, (n_blk, n_blk)))
    from_place = arrival(iota((n_blk, n_blk), 0))
    chained = (cols_down == cols) & (from_place < arrival(iota((n_blk, n_blk), 1)))
    before = jnp.max(jnp.where(chained, from_place, -1), axis=0, keepdims=True)
    final = jnp.broadcast_to(cols_down[:, :1], (n_blk, blocks)) == iota((n_blk, blocks), 1)
    last = jnp.where(final, arrival(iota((n_blk, blocks), 0)), -1)
    last = jnp.max(last, axis=0, keepdims=True)
    meta_here[...] = jnp.zeros_like(meta_here)
    meta_here[0:1, 0:n_blk] = rows_in[...]
    meta_here[1:2, 0:n_blk] = jnp.where(before < 0, n_blk, before)
    meta_here[2:3, 0:blocks] = jnp.where(last < 0, n_blk, last)

    slot = iota((slots, rows), 0)
    expert = sum((slot >= e * cap).astype(jnp.int32) for e in range(1, experts))
    place_in = (slot - expert * cap).astype(F32)
    earlier = (iota((rows, rows), 0) < iota((rows, rows), 1)).astype(F32).astype(BF16)
    for m in range(micro):
        named = [ids[m, j:j + 1, :] == expert for j in range(TOP)]
        hit = functools.reduce(jnp.logical_or, named)
        ahead = jnp.dot(
            hit.astype(F32).astype(BF16), earlier, preferred_element_type=F32
        )
        fits = hit & (ahead == place_in)
        amount = sum(jnp.where(named[j], mix[m, j:j + 1, :], 0.0) for j in range(TOP))
        disp[m] = fits.astype(F32).astype(BF16)
        comb[m] = jnp.transpose(jnp.where(fits, amount, 0.0))

    pl.semaphore_wait(barrier, sum(n - 1 for n in sizes.values()))
    meta_own.start()

    def token_copy(m):
        return pltpu.make_async_copy(tokens.at[m], held.at[m], tok_sem.at[m])

    def hand_copy(m):
        return remote(
            out.at[m], held.at[m], hand_sem.at[0, m], hand_sem.at[1, m], "section",
            peer("section", 1),
        )

    def part(group, a, k, shard):
        return weights.at[a, shard, pl.ds(group * half + k * step, step)]

    def over_shard(a, k, by):
        i = k * 3 + a
        src = sources[a].at[pl.ds(me_g * half + k * step, step)]
        return remote(
            src, part(me_g, a, k, me_s), wx_send.at[i, by], wx_recv.at[i, by], "shard",
            peer("shard", by),
        )

    def over_groups(a, k, by, hop):
        i = k * 3 + a
        spot = part(me_g, a, k, peer("shard", shards - by))
        return remote(
            spot, spot, wy_send.at[i, by, hop], wy_recv.at[i, by, hop], "groups",
            peer("groups", hop),
        )

    def meta_over_shard(by):
        return remote(
            meta_here, meta_v.at[me_s], meta_send_sem.at[by], meta_recv_sem.at[by], "shard",
            peer("shard", by),
        )

    order = [(a, k, by) for k in range(cuts) for a in range(3) for by in range(1, shards)]

    def start_weights():
        for by in range(1, shards):
            meta_over_shard(by).start()
        for a, k, by in order:
            over_shard(a, k, by).start()

    def relay_weights(first, end):
        for a, k, by in order:
            if first <= k < end:
                over_shard(a, k, by).wait_recv()
                for hop in range(1, groups):
                    over_groups(a, k, by, hop).start()

    def finish_relay(at):
        for a, k, by in order:
            if k == at:
                for hop in range(1, groups):
                    over_groups(a, k, by, hop).wait()

    early = cuts

    def relay_in_time(first, end):
        @pl.when(me_l == 0)
        def _():
            relay_weights(first, end)

    def chunk_out(m, by):
        return remote(
            send.at[m, peer("expert", by)], recv.at[m, me_e], disp_send.at[m, by],
            disp_recv.at[m, by], "expert", peer("expert", by),
        )

    def chunk_self(m):
        return pltpu.make_async_copy(send.at[m, me_e], recv.at[m, me_e], disp_self.at[m])

    def chunk_back(m, by):
        return remote(
            ret_send.at[m, peer("expert", by)], ret_recv.at[m, me_e], back_send.at[m, by],
            back_recv.at[m, by], "expert", peer("expert", by),
        )

    def back_own(m):
        return pltpu.make_async_copy(ret_send.at[m, me_e], ret_recv.at[m, me_e], back_self.at[m])

    far_first = sorted(range(1, experts), key=lambda by: abs(by - experts // 2))

    def lanes(r):
        return pl.ds(pl.multiple_of(r * blk, blk), blk)

    def strided(r):
        return pl.ds(r, slots, stride=blocks)

    def dispatch(m):
        values = held[m].astype(F32)
        scale = lax.rsqrt(jnp.mean(values * values, axis=-1, keepdims=True) + EPS)
        normed[...] = (values * scale * gain[...]).astype(BF16)

        @pl.loop(0, blocks, unroll=8)
        def _(r):
            wide[strided(r), :] = jnp.dot(
                disp[m], normed[:, lanes(r)], preferred_element_type=F32
            )

        for e in range(experts):
            send[m, e] = wide[pl.ds(e * cap * blocks, cap * blocks), :].astype(BF16)
        for by in far_first:
            chunk_out(m, by).start()
        chunk_self(m).start()

    def segment(s, k):
        products = []
        for group in range(groups):
            for u in range(step):
                c = group * half + k * step + u
                at = (k * groups + group) * step + u
                x = wide[strided(meta_s[s, 0, c]), :].astype(BF16)
                gate = jnp.dot(x, weights[0, s, c], preferred_element_type=F32)
                up = jnp.dot(x, weights[1, s, c], preferred_element_type=F32)
                hidden = (gate / (1.0 + jnp.exp(-gate)) * up).astype(BF16)
                product = jnp.dot(hidden, weights[2, s, c], preferred_element_type=F32)
                products.append((at, c, product))
        for at, c, product in products:
            parts[s, at] = product + parts[s, meta_s[s, 1, c]]

    def expert_part(m, first):
        for by in range(1, experts):
            chunk_out(m, by).wait()
        chunk_self(m).wait()
        for e in range(experts):
            wide[pl.ds(e * cap * blocks, cap * blocks), :] = recv[m, e].astype(F32)
        if first:
            for copy in own:
                copy.wait()
            for by in range(1, shards):
                meta_over_shard(by).wait()
            meta_own.wait()
            load = pltpu.make_async_copy(meta_v, meta_s, meta_copy_sem)
            load.start()
            load.wait()

            @pl.loop(0, cuts)
            def _(k):
                segment(me_s, k)

            for k in range(cuts):
                if k == 0:
                    relay_in_time(early, min(early + 1, cuts))
                elif early + k < cuts:
                    relay_in_time(early + k, early + k + 1)
                finish_relay(k)

                @pl.loop(1, shards)
                def _(by):
                    segment(peer("shard", shards - by), k)

                if k == max(0, cuts - early - 1):
                    @pl.when((me_l == 0) & (me_l < sections - 1))
                    def _():
                        pl.semaphore_signal(
                            go_sem, inc=1, device_id={"section": peer("section", 1)},
                            device_id_type=pl.DeviceIdType.MESH,
                        )
            for a, k, by in order:
                over_shard(a, k, by).wait_send()
        else:
            @pl.loop(0, shards)
            def _(s):
                @pl.loop(0, cuts)
                def _(k):
                    segment(s, k)

        @pl.loop(0, blocks, unroll=4)
        def _(j):
            total = parts[0, meta_s[0, 2, j]]
            for s in range(1, shards):
                total = total + parts[s, meta_s[s, 2, j]]
            wide[strided(j), :] = total

        for e in range(experts):
            ret_send[m, e] = wide[pl.ds(e * cap * blocks, cap * blocks), :].astype(BF16)
        for by in far_first:
            chunk_back(m, by).start()
        back_own(m).start()

    def combine(m):
        for by in range(1, experts):
            chunk_back(m, by).wait()
        back_own(m).wait()
        for e in range(experts):
            wide[pl.ds(e * cap * blocks, cap * blocks), :] = ret_recv[m, e].astype(F32)

        @pl.loop(0, blocks, unroll=8)
        def _(r):
            mixed = jnp.dot(
                comb[m], wide[strided(r), :], preferred_element_type=F32,
                precision=lax.Precision.HIGHEST,
            )
            out[m, :, lanes(r)] = (held[m, :, lanes(r)].astype(F32) + mixed).astype(BF16)

    for s in range(shards):
        parts[s, n_blk] = jnp.zeros_like(parts[s, n_blk])

    @pl.when(me_l == 0)
    def _():
        for m in range(micro):
            token_copy(m).start()
        start_weights()
        for m in range(micro):
            token_copy(m).wait()
            dispatch(m)
        relay_weights(0, early)

    @pl.when(me_l > 0)
    def _():
        pl.semaphore_wait(go_sem, 1)
        start_weights()
        relay_weights(0, cuts)

    @pl.when((me_l > 0) & (me_l < sections - 1))
    def _():
        pl.semaphore_signal(
            go_sem, inc=1, device_id={"section": peer("section", 1)},
            device_id_type=pl.DeviceIdType.MESH,
        )

    @pl.when(me_l > 0)
    def _():
        for m in range(micro):
            hand_copy(m).wait_recv()
            dispatch(m)

    for m in range(micro):
        expert_part(m, m == 0)
    for m in range(micro):
        combine(m)

        @pl.when(me_l < sections - 1)
        def _():
            hand_copy(m).start()

    @pl.when(me_l < sections - 1)
    def _():
        for m in range(micro):
            hand_copy(m).wait_send()


def body(
    sizes,
    tokens,
    norm_gain,
    route_ids,
    route_weights,
    gate_blocks,
    up_blocks,
    down_blocks,
    gate_rows,
    down_cols,
):
    groups, shards, experts, sections = sizes
    micro, rows, width = tokens.shape
    n_blk, blk = gate_blocks.shape[2], gate_blocks.shape[-1]
    blocks = width // blk
    cap = min(rows, max(rows * 9 // 16, rows * TOP // experts + 2))
    slots = experts * cap

    cuts = math.gcd(n_blk // groups, 4)
    meta_width = -(-max(n_blk, blocks) // 128) * 128
    pieces = 3 * cuts
    dims = (micro, rows, blocks, blk, cap, experts, shards, groups, sections, n_blk)
    dma = pltpu.SemaphoreType.DMA
    chunk = (micro, experts, cap * blocks, blk)
    vmem, anywhere = pl.BlockSpec(memory_space=pltpu.VMEM), pl.BlockSpec(memory_space=pl.ANY)
    out = pl.pallas_call(
        functools.partial(layer_kernel, dims),
        out_shape=jax.ShapeDtypeStruct((micro, rows, width), BF16),
        in_specs=[anywhere] + [vmem] * 3 + [anywhere] * 3 + [vmem] * 2,
        out_specs=vmem,
        scratch_shapes=[
            pltpu.VMEM((micro, rows, width), BF16),
            pltpu.VMEM((micro, slots, rows), BF16),
            pltpu.VMEM((micro, rows, slots), F32),
            pltpu.VMEM((8, meta_width), jnp.int32),
            pltpu.VMEM((rows, width), BF16),
            pltpu.VMEM((slots * blocks, blk), F32),
            pltpu.VMEM(chunk, BF16),
            pltpu.VMEM(chunk, BF16),
            pltpu.VMEM((shards, n_blk + 1, slots, blk), F32),
            pltpu.VMEM(chunk, BF16),
            pltpu.VMEM(chunk, BF16),
            pltpu.VMEM((3, shards, n_blk, blk, blk), BF16),
            pltpu.VMEM((shards, 8, meta_width), jnp.int32),
            pltpu.SMEM((shards, 8, meta_width), jnp.int32),
            dma((micro,)),
            dma((2, micro)),
            dma((3,)),
            dma,
            dma((shards,)),
            dma((shards,)),
            dma,
            dma((pieces, shards)),
            dma((pieces, shards)),
            dma((pieces, shards, groups)),
            dma((pieces, shards, groups)),
            dma((micro, experts)),
            dma((micro, experts)),
            dma((micro,)),
            dma((micro, experts)),
            dma((micro, experts)),
            dma((micro,)),
            pltpu.SemaphoreType.REGULAR,
        ],
        compiler_params=pltpu.CompilerParams(
            collective_id=0, has_side_effects=True, vmem_limit_bytes=56 * 1024 * 1024
        ),
    )(
        tokens, norm_gain, jnp.swapaxes(route_ids[0], 1, 2), jnp.swapaxes(route_weights[0], 1, 2),
        gate_blocks.reshape(n_blk, blk, blk), up_blocks.reshape(n_blk, blk, blk),
        down_blocks.reshape(n_blk, blk, blk), gate_rows.reshape(1, n_blk),
        down_cols.reshape(1, n_blk),
    )
    return out[None]


def solution(mesh):
    sizes = tuple(mesh.shape[name] for name in ("groups", "shard", "expert", "section"))
    in_specs = (
        P(None, ("groups", "shard", "expert"), None),
        P("section", None),
        P("section", None, ("groups", "shard", "expert"), None),
        P("section", None, ("groups", "shard", "expert"), None),
        P("section", "expert", "shard", None, None, None),
        P("section", "expert", "shard", None, None, None),
        P("section", "expert", "shard", None, None, None),
        P("section", "expert", "shard", None),
        P("section", "expert", "shard", None),
    )
    out_specs = P("section", None, ("groups", "shard", "expert"), None)
    return jax.shard_map(
        functools.partial(body, sizes), mesh=mesh, in_specs=in_specs, out_specs=out_specs,
        check_vma=False,
    )
```

```python
import functools
import math

import jax
import jax.numpy as jnp
from jax import lax
from jax.experimental import pallas as pl
from jax.experimental.pallas import tpu as pltpu
from jax.sharding import PartitionSpec as P

TOP = 2
EPS = 1e-05
BF16 = jnp.bfloat16
F32 = jnp.float32


def layer_kernel(
    dims,
    tokens, gain, ids, mix, gate_hbm, up_hbm, down_hbm, rows_in, cols_in,
    out,
    held, disp, comb, meta_here, normed, wide, send, recv, parts, ret_send, ret_recv, weights, meta_v, meta_s,
    tok_sem, hand_sem, own_sem, meta_own_sem, meta_send_sem, meta_recv_sem, meta_copy_sem,
    wx_send, wx_recv, wy_send, wy_recv, disp_send, disp_recv, disp_self,
    back_send, back_recv, back_self, go_sem,
):
    micro, rows, blocks, blk, cap, experts, shards, groups, sections, n_blk = dims
    slots = experts * cap
    me_g, me_s = lax.axis_index("groups"), lax.axis_index("shard")
    me_e, me_l = lax.axis_index("expert"), lax.axis_index("section")
    sizes = {"groups": groups, "shard": shards, "expert": experts, "section": sections}
    place = {"groups": me_g, "shard": me_s, "expert": me_e, "section": me_l}
    half = n_blk // groups
    cuts = math.gcd(half, 4)
    step = half // cuts
    sources = (gate_hbm, up_hbm, down_hbm)

    def remote(src, dst, ssem, rsem, axis, index):
        return pltpu.make_async_remote_copy(
            src_ref=src, dst_ref=dst, send_sem=ssem, recv_sem=rsem,
            device_id={axis: index}, device_id_type=pl.DeviceIdType.MESH,
        )

    def peer(axis, by):
        return lax.rem(place[axis] + by, sizes[axis])

    own = [
        pltpu.make_async_copy(sources[a], weights.at[a, me_s], own_sem.at[a]) for a in range(3)
    ]
    for copy in own:
        copy.start()

    def token_copy(m):
        return pltpu.make_async_copy(tokens.at[m], held.at[m], tok_sem.at[m])

    @pl.when(me_l == 0)
    def _():
        for m in range(micro):
            token_copy(m).start()

    meta_own = pltpu.make_async_copy(meta_here, meta_v.at[me_s], meta_own_sem)

    barrier = pltpu.get_barrier_semaphore()
    for axis in ("groups", "shard", "expert", "section"):
        for by in range(1, sizes[axis]):
            pl.semaphore_signal(
                barrier, inc=1, device_id={axis: peer(axis, by)},
                device_id_type=pl.DeviceIdType.MESH,
            )

    pl.semaphore_wait(barrier, sum(n - 1 for n in sizes.values()))

    def hand_copy(m):
        return remote(
            out.at[m], held.at[m], hand_sem.at[0, m], hand_sem.at[1, m], "section",
            peer("section", 1),
        )

    def part(group, a, k, shard):
        return weights.at[a, shard, pl.ds(group * half + k * step, step)]

    def over_shard(a, k, by):
        i = k * 3 + a
        src = sources[a].at[pl.ds(me_g * half + k * step, step)]
        return remote(
            src, part(me_g, a, k, me_s), wx_send.at[i, by], wx_recv.at[i, by], "shard",
            peer("shard", by),
        )

    def over_groups(a, k, by, hop):
        i = k * 3 + a
        spot = part(me_g, a, k, peer("shard", shards - by))
        return remote(
            spot, spot, wy_send.at[i, by, hop], wy_recv.at[i, by, hop], "groups",
            peer("groups", hop),
        )

    def meta_over_shard(by):
        return remote(
            meta_here, meta_v.at[me_s], meta_send_sem.at[by], meta_recv_sem.at[by], "shard",
            peer("shard", by),
        )

    order = [(a, k, by) for k in range(cuts) for a in range(3) for by in range(1, shards)]

    def start_weights():
        for a, k, by in order:
            over_shard(a, k, by).start()

    def relay_weights(first, end):
        for a, k, by in order:
            if first <= k < end:
                over_shard(a, k, by).wait_recv()
                for hop in range(1, groups):
                    over_groups(a, k, by, hop).start()

    def finish_relay(at):
        for a, k, by in order:
            if k == at:
                for hop in range(1, groups):
                    over_groups(a, k, by, hop).wait()

    early = cuts

    def relay_in_time(first, end):
        @pl.when(me_l == 0)
        def _():
            relay_weights(first, end)

    def chunk_out(m, by):
        return remote(
            send.at[m, peer("expert", by)], recv.at[m, me_e], disp_send.at[m, by],
            disp_recv.at[m, by], "expert", peer("expert", by),
        )

    def chunk_self(m):
        return pltpu.make_async_copy(send.at[m, me_e], recv.at[m, me_e], disp_self.at[m])

    def chunk_back(m, by):
        return remote(
            ret_send.at[m, peer("expert", by)], ret_recv.at[m, me_e], back_send.at[m, by],
            back_recv.at[m, by], "expert", peer("expert", by),
        )

    def back_own(m):
        return pltpu.make_async_copy(ret_send.at[m, me_e], ret_recv.at[m, me_e], back_self.at[m])

    far_first = sorted(range(1, experts), key=lambda by: abs(by - experts // 2))

    def lanes(r):
        return pl.ds(pl.multiple_of(r * blk, blk), blk)

    def chunk_rows(e):
        return pl.ds(pl.multiple_of(e * (cap * blocks), 16), cap * blocks)

    def strided(r):
        return pl.ds(r, slots, stride=blocks)

    def dispatch(m):
        values = held[m].astype(F32)
        scale = lax.rsqrt(jnp.mean(values * values, axis=-1, keepdims=True) + EPS)
        normed[...] = (values * scale * gain[...]).astype(BF16)

        @pl.loop(0, blocks, unroll=8)
        def _(r):
            wide[strided(r), :] = jnp.dot(
                disp[m], normed[:, lanes(r)], preferred_element_type=F32
            )

        for by in far_first + [0]:
            e = peer("expert", by)
            send[m, e] = wide[chunk_rows(e), :].astype(BF16)
            if by > 0:
                chunk_out(m, by).start()
        chunk_self(m).start()

    def segment(s, k):
        products = []
        for group in range(groups):
            for u in range(step):
                c = group * half + k * step + u
                at = (k * groups + group) * step + u
                x = wide[strided(meta_s[s, 0, c]), :].astype(BF16)
                gate = jnp.dot(x, weights[0, s, c], preferred_element_type=F32)
                up = jnp.dot(x, weights[1, s, c], preferred_element_type=F32)
                hidden = (gate / (1.0 + jnp.exp(-gate)) * up).astype(BF16)
                product = jnp.dot(hidden, weights[2, s, c], preferred_element_type=F32)
                products.append((at, c, product))
        for at, c, product in products:
            parts[s, at] = product + parts[s, meta_s[s, 1, c]]

    def expert_part(m, first):
        chunk_self(m).wait()
        wide[chunk_rows(me_e), :] = recv[m, me_e].astype(F32)
        for by in far_first:
            chunk_out(m, by).wait()
            e = peer("expert", experts - by)
            wide[chunk_rows(e), :] = recv[m, e].astype(F32)
        if first:
            for copy in own:
                copy.wait()
            for by in range(1, shards):
                meta_over_shard(by).wait()
            meta_own.wait()
            load = pltpu.make_async_copy(meta_v, meta_s, meta_copy_sem)
            load.start()
            load.wait()

            @pl.loop(0, cuts)
            def _(k):
                segment(me_s, k)

            for k in range(cuts):
                if k == 0:
                    relay_in_time(early, min(early + 1, cuts))
                elif early + k < cuts:
                    relay_in_time(early + k, early + k + 1)
                finish_relay(k)

                @pl.loop(1, shards)
                def _(by):
                    segment(peer("shard", shards - by), k)

                if k == max(0, cuts - early - 1):
                    @pl.when((me_l == 0) & (me_l < sections - 1))
                    def _():
                        pl.semaphore_signal(
                            go_sem, inc=1, device_id={"section": peer("section", 1)},
                            device_id_type=pl.DeviceIdType.MESH,
                        )
            for a, k, by in order:
                over_shard(a, k, by).wait_send()
        else:
            @pl.loop(0, shards)
            def _(s):
                @pl.loop(0, cuts)
                def _(k):
                    segment(s, k)

        @pl.loop(0, blocks, unroll=4)
        def _(j):
            total = parts[0, meta_s[0, 2, j]]
            for s in range(1, shards):
                total = total + parts[s, meta_s[s, 2, j]]
            wide[strided(j), :] = total

        for by in far_first + [0]:
            e = peer("expert", by)
            ret_send[m, e] = wide[chunk_rows(e), :].astype(BF16)
            if by > 0:
                chunk_back(m, by).start()
        back_own(m).start()

    def combine(m):
        back_own(m).wait()
        wide[chunk_rows(me_e), :] = ret_recv[m, me_e].astype(F32)
        for by in far_first:
            chunk_back(m, by).wait()
            e = peer("expert", experts - by)
            wide[chunk_rows(e), :] = ret_recv[m, e].astype(F32)

        @pl.loop(0, blocks, unroll=8)
        def _(r):
            mixed = jnp.dot(
                comb[m], wide[strided(r), :], preferred_element_type=F32,
                precision=lax.Precision.HIGHEST,
            )
            out[m, :, lanes(r)] = (held[m, :, lanes(r)].astype(F32) + mixed).astype(BF16)

    @pl.when(me_l == 0)
    def _():
        start_weights()

    def arrival(c):
        group = sum((c >= g * half).astype(jnp.int32) for g in range(1, groups))
        within = c - group * half
        k = sum((within >= i * step).astype(jnp.int32) for i in range(1, cuts))
        return k * (groups - 1) * step + group * step + within

    def iota(shape, axis):
        return lax.broadcasted_iota(jnp.int32, shape, axis)

    cols = cols_in[...]
    cols_down = jnp.transpose(jnp.broadcast_to(cols, (n_blk, n_blk)))
    from_place = arrival(iota((n_blk, n_blk), 0))
    chained = (cols_down == cols) & (from_place < arrival(iota((n_blk, n_blk), 1)))
    before = jnp.max(jnp.where(chained, from_place, -1), axis=0, keepdims=True)
    final = jnp.broadcast_to(cols_down[:, :1], (n_blk, blocks)) == iota((n_blk, blocks), 1)
    last = jnp.where(final, arrival(iota((n_blk, blocks), 0)), -1)
    last = jnp.max(last, axis=0, keepdims=True)
    meta_here[...] = jnp.zeros_like(meta_here)
    meta_here[0:1, 0:n_blk] = rows_in[...]
    meta_here[1:2, 0:n_blk] = jnp.where(before < 0, n_blk, before)
    meta_here[2:3, 0:blocks] = jnp.where(last < 0, n_blk, last)

    slot = iota((slots, rows), 0)
    expert = sum((slot >= e * cap).astype(jnp.int32) for e in range(1, experts))
    place_in = (slot - expert * cap).astype(F32)
    earlier = (iota((rows, rows), 0) < iota((rows, rows), 1)).astype(F32).astype(BF16)
    for m in range(micro):
        named = [ids[m, j:j + 1, :] == expert for j in range(TOP)]
        hit = functools.reduce(jnp.logical_or, named)
        ahead = jnp.dot(
            hit.astype(F32).astype(BF16), earlier, preferred_element_type=F32
        )
        fits = hit & (ahead == place_in)
        amount = sum(jnp.where(named[j], mix[m, j:j + 1, :], 0.0) for j in range(TOP))
        disp[m] = fits.astype(F32).astype(BF16)
        comb[m] = jnp.transpose(jnp.where(fits, amount, 0.0))

    meta_own.start()
    for by in range(1, shards):
        meta_over_shard(by).start()
    for s in range(shards):
        parts[s, n_blk] = jnp.zeros_like(parts[s, n_blk])

    @pl.when(me_l == 0)
    def _():
        for m in range(micro):
            token_copy(m).wait()
            dispatch(m)
        relay_weights(0, early)

    @pl.when(me_l > 0)
    def _():
        pl.semaphore_wait(go_sem, 1)
        start_weights()
        relay_weights(0, cuts)

    @pl.when((me_l > 0) & (me_l < sections - 1))
    def _():
        pl.semaphore_signal(
            go_sem, inc=1, device_id={"section": peer("section", 1)},
            device_id_type=pl.DeviceIdType.MESH,
        )

    @pl.when(me_l > 0)
    def _():
        for m in range(micro):
            hand_copy(m).wait_recv()
            dispatch(m)

    for m in range(micro):
        expert_part(m, m == 0)
    for m in range(micro):
        combine(m)

        @pl.when(me_l < sections - 1)
        def _():
            hand_copy(m).start()

    @pl.when(me_l < sections - 1)
    def _():
        for m in range(micro):
            hand_copy(m).wait_send()


def body(
    sizes,
    tokens,
    norm_gain,
    route_ids,
    route_weights,
    gate_blocks,
    up_blocks,
    down_blocks,
    gate_rows,
    down_cols,
):
    groups, shards, experts, sections = sizes
    micro, rows, width = tokens.shape
    n_blk, blk = gate_blocks.shape[2], gate_blocks.shape[-1]
    blocks = width // blk
    cap = min(rows, max(rows * 9 // 16, rows * TOP // experts + 2))
    slots = experts * cap

    cuts = math.gcd(n_blk // groups, 4)
    meta_width = -(-max(n_blk, blocks) // 128) * 128
    pieces = 3 * cuts
    dims = (micro, rows, blocks, blk, cap, experts, shards, groups, sections, n_blk)
    dma = pltpu.SemaphoreType.DMA
    chunk = (micro, experts, cap * blocks, blk)
    vmem, anywhere = pl.BlockSpec(memory_space=pltpu.VMEM), pl.BlockSpec(memory_space=pl.ANY)
    out = pl.pallas_call(
        functools.partial(layer_kernel, dims),
        out_shape=jax.ShapeDtypeStruct((micro, rows, width), BF16),
        in_specs=[anywhere] + [vmem] * 3 + [anywhere] * 3 + [vmem] * 2,
        out_specs=vmem,
        scratch_shapes=[
            pltpu.VMEM((micro, rows, width), BF16),
            pltpu.VMEM((micro, slots, rows), BF16),
            pltpu.VMEM((micro, rows, slots), F32),
            pltpu.VMEM((8, meta_width), jnp.int32),
            pltpu.VMEM((rows, width), BF16),
            pltpu.VMEM((slots * blocks, blk), F32),
            pltpu.VMEM(chunk, BF16),
            pltpu.VMEM(chunk, BF16),
            pltpu.VMEM((shards, n_blk + 1, slots, blk), F32),
            pltpu.VMEM(chunk, BF16),
            pltpu.VMEM(chunk, BF16),
            pltpu.VMEM((3, shards, n_blk, blk, blk), BF16),
            pltpu.VMEM((shards, 8, meta_width), jnp.int32),
            pltpu.SMEM((shards, 8, meta_width), jnp.int32),
            dma((micro,)),
            dma((2, micro)),
            dma((3,)),
            dma,
            dma((shards,)),
            dma((shards,)),
            dma,
            dma((pieces, shards)),
            dma((pieces, shards)),
            dma((pieces, shards, groups)),
            dma((pieces, shards, groups)),
            dma((micro, experts)),
            dma((micro, experts)),
            dma((micro,)),
            dma((micro, experts)),
            dma((micro, experts)),
            dma((micro,)),
            pltpu.SemaphoreType.REGULAR,
        ],
        compiler_params=pltpu.CompilerParams(
            collective_id=0, has_side_effects=True, vmem_limit_bytes=56 * 1024 * 1024
        ),
    )(
        tokens, norm_gain, jnp.swapaxes(route_ids[0], 1, 2), jnp.swapaxes(route_weights[0], 1, 2),
        gate_blocks.reshape(n_blk, blk, blk), up_blocks.reshape(n_blk, blk, blk),
        down_blocks.reshape(n_blk, blk, blk), gate_rows.reshape(1, n_blk),
        down_cols.reshape(1, n_blk),
    )
    return out[None]


def solution(mesh):
    sizes = tuple(mesh.shape[name] for name in ("groups", "shard", "expert", "section"))
    in_specs = (
        P(None, ("groups", "shard", "expert"), None),
        P("section", None),
        P("section", None, ("groups", "shard", "expert"), None),
        P("section", None, ("groups", "shard", "expert"), None),
        P("section", "expert", "shard", None, None, None),
        P("section", "expert", "shard", None, None, None),
        P("section", "expert", "shard", None, None, None),
        P("section", "expert", "shard", None),
        P("section", "expert", "shard", None),
    )
    out_specs = P("section", None, ("groups", "shard", "expert"), None)
    return jax.shard_map(
        functools.partial(body, sizes), mesh=mesh, in_specs=in_specs, out_specs=out_specs,
        check_vma=False,
    )
```
